768 devices in a mesh: section: 12 (over z_hi, x), tm: 8 (over z_lo, core), space: 8 (over y).
Axes of the slice: x: 4, y: 8, z: 12 (z_hi: 3, z_lo: 4; z = z_hi * 4 + z_lo), core: 2. Of those that a mesh axis runs over, the one named last changes fastest.
Arguments:
- video: bfloat16 [12, 16, 512, 1152], P('section', 'tm', 'space'), may hold values from -6 to 6
- conv_taps: float32 [12, 3, 1152], P('section'), may hold values from -3 to 3
- modulation: float32 [12, 6, 1152], P('section'), may hold values from -3 to 3
- w_qkv: bfloat16 [12, 1152, 3, 1152], P('section', None, None, 'space'), may hold values from -6 to 6
- w_out: bfloat16 [12, 1152, 1152], P('section', 'space'), may hold values from -0.1875 to 0.1875
- w_up: bfloat16 [12, 1152, 4608], P('section', None, 'space'), may hold values from -0.1875 to 0.1875
- w_down: bfloat16 [12, 4608, 1152], P('section', 'space'), may hold values from -0.09375 to 0.09375
Outputs:
- next_in: bfloat16 [12, 16, 512, 1152], P('section', 'tm', 'space')
The draws below stay inside these ranges and needn't reach their ends.
All inputs are finite; a program needn't handle non-finite values.
Results may differ from the reference program's by a relative error of at most 0.013.
Values may be sent and summed in bfloat16 or wider, within the bound.
No kernel may reach another device: no remote copies, remote signals or barrier semaphores. Data moves between devices by JAX's collectives and lax.ppermute only.
A program may use at most 32 MiB of HBM per device.

```python
import math
import jax
import jax.numpy as jnp
from jax import lax

D = 1152
HEADS = 16
FF = 4608
LAYERS = 12
FRAMES = 16
HW = 512
N_SPACE = 8


def draw_w_qkv(key, part):
    sampled = jax.random.truncated_normal(key, -5.0, 5.0, (LAYERS, D, 3, D), jnp.float32) / jnp.sqrt(jnp.float32(D))
    return sampled.astype(jnp.bfloat16)


def level_of(key, extent, shards, low, high):
    level, own = 1.0, jax.random.fold_in(key, 6)
    for position, parts in shards:
        heights = jnp.exp(jax.random.uniform(jax.random.fold_in(own, position), (parts,), jnp.float32, low / len(shards), high / len(shards)))
        level = level * jnp.repeat(heights, extent[position] // parts).reshape([-1 if axis == position else 1 for axis in range(len(extent))])
    return level


def scatter_about(rng, shape, spread, most, cuts=(), dtype=jnp.bfloat16):
    gain = level_of(rng, shape, cuts, -0.22, 0.18) if cuts else 1.0
    drawn = jax.random.normal(rng, shape, jnp.float32) * spread * gain
    return jnp.minimum(jnp.maximum(drawn, -most), most).astype(dtype)


def setup_inputs(seed: int = 0) -> dict:
    splits = jax.random.split(jax.random.key(seed), 8)
    video = scatter_about(splits[0], (LAYERS, FRAMES, HW, D), 1.0, 6.0, ((0, 12), (1, 8), (2, 8)))
    conv_taps = scatter_about(splits[1], (LAYERS, 3, D), 0.5, 3.0, ((0, 12),), jnp.float32)
    modulation = scatter_about(splits[2], (LAYERS, 6, D), 0.5, 3.0, ((0, 12),), jnp.float32)
    w_qkv = draw_w_qkv(jax.random.fold_in(splits[7], 71), 0)
    w_out = scatter_about(splits[4], (LAYERS, D, D), D ** -0.5, 0.1875, ((0, 12), (1, 8)))
    w_up = scatter_about(splits[5], (LAYERS, D, FF), D ** -0.5, 0.1875, ((0, 12), (2, 8)))
    w_down = scatter_about(splits[6], (LAYERS, FF, D), FF ** -0.5, 0.09375, ((0, 12), (1, 8)))
    return dict(video=video, conv_taps=conv_taps, modulation=modulation, w_qkv=w_qkv, w_out=w_out, w_up=w_up, w_down=w_down)


def normalize(values_in):
    centre = lax.optimization_barrier(jnp.mean(values_in, axis=-1, keepdims=True))
    variance = lax.optimization_barrier(jnp.mean(jnp.square(values_in - centre), axis=-1, keepdims=True))
    return (values_in - centre) * lax.rsqrt(variance + 1e-06)

def modulated(values_in, shift_row, scale_row):
    return (normalize(values_in) * (1.0 + scale_row) + shift_row).astype(jnp.bfloat16)

def one_layer(slices):
    frames_in, tap_set, mod_table, query_w, out_w, up_w, down_w = slices
    frames_f32 = frames_in.astype(jnp.float32)
    padded = jnp.concatenate([jnp.zeros((2,) + frames_f32.shape[1:], jnp.float32), frames_f32], axis=0)
    conv_sum = tap_set[0] * padded[2:] + tap_set[1] * padded[1:-1] + tap_set[2] * padded[:-2]
    mixed_rows = (frames_f32 + conv_sum).astype(jnp.bfloat16)
    head_size = D // HEADS
    group_cols = D // N_SPACE
    group_ff = FF // N_SPACE

    def one_frame(frame_rows):
        frame_f32 = frame_rows.astype(jnp.float32)
        attn_in = modulated(frame_f32, mod_table[0], mod_table[1])
        projected = jnp.dot(attn_in, query_w.reshape(D, 3 * D), preferred_element_type=jnp.float32).astype(jnp.bfloat16)
        projected = projected.reshape(HW, 3, HEADS, head_size).astype(jnp.float32)
        scores = jnp.einsum('qhe,khe->hqk', projected[:, 0], projected[:, 1]) * (1.0 / math.sqrt(head_size))
        probs = jax.nn.softmax(scores, axis=-1).astype(jnp.bfloat16)
        heads_out = jnp.einsum('hqk,khe->qhe', probs.astype(jnp.float32), projected[:, 2]).astype(jnp.bfloat16)
        heads_out = heads_out.reshape(HW, N_SPACE, group_cols).astype(jnp.float32)
        grouped = jnp.einsum('qgk,gkd->gqd', heads_out, out_w.reshape(N_SPACE, group_cols, D).astype(jnp.float32))
        attn_sum = lax.optimization_barrier(jnp.sum(grouped.astype(jnp.bfloat16).astype(jnp.float32), axis=0))
        hidden_state = frame_f32 + mod_table[2] * attn_sum
        mlp_in = modulated(hidden_state, mod_table[3], mod_table[4])
        activated = jax.nn.gelu(jnp.dot(mlp_in, up_w, preferred_element_type=jnp.float32), approximate=True).astype(jnp.bfloat16)
        activated = activated.reshape(HW, N_SPACE, group_ff).astype(jnp.float32)
        grouped_mlp = jnp.einsum('qgk,gkd->gqd', activated, down_w.reshape(N_SPACE, group_ff, D).astype(jnp.float32))
        mlp_sum = lax.optimization_barrier(jnp.sum(grouped_mlp.astype(jnp.bfloat16).astype(jnp.float32), axis=0))
        return (hidden_state + mod_table[5] * mlp_sum).astype(jnp.bfloat16)
    return lax.map(one_frame, mixed_rows)

def reference(video, conv_taps, modulation, w_qkv, w_out, w_up, w_down):
    layer_out = lax.map(one_layer, (video, conv_taps, modulation, w_qkv, w_out, w_up, w_down))
    return jnp.roll(layer_out, 1, axis=0)
```

```python
import math

import jax
import jax.numpy as jnp
from jax import lax
from jax.sharding import PartitionSpec as P

D = 1152
HEADS = 16
HEAD = D // HEADS
BF16 = jnp.bfloat16
F32 = jnp.float32


def shifted(value, axis, steps):
    count = lax.axis_size(axis)
    initial, last = (max(0, -steps), min(count, count - steps))
    return lax.ppermute(value, axis, [(source, source + steps) for source in range(initial, last)])


def rotate(block, axis, steps):
    count = lax.axis_size(axis)
    return lax.ppermute(block, axis, [(i, (i + steps) % count) for i in range(count)])


def flip(block, axis):
    return lax.ppermute(block, axis, [(i, i ^ 1) for i in range(lax.axis_size(axis))])


def turn_z(block, steps):
    count = lax.axis_size("tm")
    return lax.ppermute(block, "tm", [(i, (i + 2 * steps) % count) for i in range(count)])


def normalize(values_in):
    centre = jnp.mean(values_in, axis=-1, keepdims=True)
    variance = jnp.mean(jnp.square(values_in - centre), axis=-1, keepdims=True)
    return (values_in - centre) * lax.rsqrt(variance + 1e-06)


def modulated(values_in, shift_row, scale_row):
    return (normalize(values_in) * (1.0 + scale_row) + shift_row).astype(BF16)


def attend(rows, qkv, out_w):
    tokens, heads = rows.shape[0], qkv.shape[1] // HEAD
    projected = jnp.einsum("te,cne->tcn", rows, qkv, preferred_element_type=F32).astype(BF16)
    projected = projected.reshape(tokens, 3, heads, HEAD)
    scores = jnp.einsum(
        "qhe,khe->hqk", projected[:, 0], projected[:, 1], preferred_element_type=F32
    ) * (1.0 / math.sqrt(HEAD))
    probs = jax.nn.softmax(scores, axis=-1).astype(BF16)
    heads_out = jnp.einsum("hqk,khe->qhe", probs, projected[:, 2], preferred_element_type=F32)
    heads_out = heads_out.astype(BF16).reshape(tokens, heads * HEAD)
    return jnp.dot(heads_out, out_w, preferred_element_type=F32)


def feed_forward(rows, up_w, down_w):
    activated = jax.nn.gelu(
        jnp.einsum("te,ne->tn", rows, up_w, preferred_element_type=F32), approximate=True
    ).astype(BF16)
    return jnp.dot(activated, down_w, preferred_element_type=F32)


def far_shards(up_w, down_w):
    place, members = lax.axis_index("tm"), lax.axis_size("tm")
    share = up_w.shape[0] // members
    piece = jnp.concatenate(
        [lax.dynamic_slice_in_dim(w, place * share, share, 0) for w in (up_w, down_w)], axis=0
    )
    piece = rotate(piece, "space", lax.axis_size("space") // 2)
    along = [piece] + [turn_z(piece, k) for k in range(1, members // 2)]
    mine = jnp.stack(along)
    pieces = jnp.concatenate([mine, flip(mine, "tm")], axis=0)
    return pieces[:, :share].reshape(-1, D), pieces[:, share:].reshape(-1, D)


def body(video, conv_taps, modulation, w_qkv, w_out, w_up, w_down):
    frames_in = video[0]
    tap_set = conv_taps[0]
    mod_table = modulation[0]
    frames, tokens = frames_in.shape[:2]
    n_space = lax.axis_size("space")
    qkv_own = w_qkv[0].transpose(1, 2, 0)
    out_own = w_out[0]
    up_own = w_up[0].T
    down_own = w_down[0]

    earlier = shifted(frames_in, "tm", 1)
    qkv_near = flip(qkv_own, "space")
    out_near = flip(out_own, "space")
    up_far, down_far = far_shards(up_own, down_own)

    extended = jnp.concatenate([earlier, frames_in], axis=0).astype(F32)
    mixed_rows = (
        extended[2:]
        + tap_set[0] * extended[2:]
        + tap_set[1] * extended[1:-1]
        + tap_set[2] * extended[:-2]
    ).astype(BF16)
    mixed_f32 = mixed_rows.astype(F32)

    attn_in = modulated(mixed_f32, mod_table[0], mod_table[1])
    outgoing = jnp.broadcast_to(attn_in[None], (n_space // frames, frames, tokens, D))
    rows = lax.all_to_all(outgoing.reshape(n_space, tokens, D), "space", 0, 0, tiled=True)
    rows = rows.reshape(n_space * tokens, D)
    attn_part = attend(rows, qkv_own, out_own) + attend(rows, qkv_near, out_near)
    attn_part = attn_part.astype(BF16).reshape(n_space, tokens, D)
    parts = lax.all_to_all(attn_part, "space", 0, 0, tiled=True)
    attn_sum = jnp.sum(parts.reshape(n_space // frames, frames, tokens, D).astype(F32), axis=0)
    hidden_state = mixed_f32 + mod_table[2] * attn_sum

    mlp_in = modulated(hidden_state, mod_table[3], mod_table[4])
    visitors = [
        mlp_in,
        rotate(mlp_in, "space", 1),
        rotate(mlp_in, "space", -1),
        rotate(mlp_in[:1], "space", 2),
        rotate(mlp_in[1:], "space", -2),
    ]
    mlp_rows = jnp.concatenate(visitors, axis=0).reshape(-1, D)
    mlp_part = feed_forward(mlp_rows, up_own, down_own) + feed_forward(mlp_rows, up_far, down_far)
    mlp_part = mlp_part.astype(BF16).reshape(-1, tokens, D)
    back = [
        rotate(mlp_part[2:4], "space", -1),
        rotate(mlp_part[4:6], "space", 1),
        jnp.concatenate(
            [rotate(mlp_part[6:7], "space", -2), rotate(mlp_part[7:8], "space", 2)], axis=0
        ),
    ]
    mlp_sum = mlp_part[:2].astype(F32) + sum(part.astype(F32) for part in back)
    layer_out = (hidden_state + mod_table[5] * mlp_sum).astype(BF16)
    return rotate(layer_out, "section", 1)[None]


def solution(mesh):
    placed = (
        P("section", "tm", "space", None),
        P("section", None, None),
        P("section", None, None),
        P("section", None, None, "space"),
        P("section", "space", None),
        P("section", None, "space"),
        P("section", "space", None),
    )
    return jax.shard_map(
        body,
        mesh=mesh,
        in_specs=placed,
        out_specs=P("section", "tm", "space", None),
        check_vma=False,
    )
```

```python
import math

import jax
import jax.numpy as jnp
from jax import lax
from jax.sharding import PartitionSpec as P

D = 1152
HEADS = 16
HEAD = D // HEADS
BF16 = jnp.bfloat16
F32 = jnp.float32


def shifted(value, axis, steps):
    count = lax.axis_size(axis)
    initial, last = (max(0, -steps), min(count, count - steps))
    return lax.ppermute(value, axis, [(source, source + steps) for source in range(initial, last)])


def rotate(block, axis, steps):
    count = lax.axis_size(axis)
    return lax.ppermute(block, axis, [(i, (i + steps) % count) for i in range(count)])


def flip(block, axis):
    return lax.ppermute(block, axis, [(i, i ^ 1) for i in range(lax.axis_size(axis))])


def turn_z(block, steps):
    count = lax.axis_size("tm")
    return lax.ppermute(block, "tm", [(i, (i + 2 * steps) % count) for i in range(count)])


def normalize(values_in):
    centre = jnp.mean(values_in, axis=-1, keepdims=True)
    variance = jnp.mean(jnp.square(values_in - centre), axis=-1, keepdims=True)
    return (values_in - centre) * lax.rsqrt(variance + 1e-06)


def modulated(values_in, shift_row, scale_row):
    return (normalize(values_in) * (1.0 + scale_row) + shift_row).astype(BF16)


def attend(rows, qkv, out_w):
    tokens, heads = rows.shape[0], qkv.shape[1] // HEAD
    projected = jnp.einsum("te,cne->tcn", rows, qkv, preferred_element_type=F32).astype(BF16)
    projected = projected.reshape(tokens, 3, heads, HEAD)
    scores = jnp.einsum(
        "qhe,khe->hqk", projected[:, 0], projected[:, 1], preferred_element_type=F32
    ) * (1.0 / math.sqrt(HEAD))
    probs = jax.nn.softmax(scores, axis=-1).astype(BF16)
    heads_out = jnp.einsum("hqk,khe->qhe", probs, projected[:, 2], preferred_element_type=F32)
    heads_out = heads_out.astype(BF16).reshape(tokens, heads * HEAD)
    return jnp.dot(heads_out, out_w, preferred_element_type=F32)


def feed_forward(rows, up_w, down_w):
    activated = jax.nn.gelu(
        jnp.einsum("te,ne->tn", rows, up_w, preferred_element_type=F32), approximate=True
    ).astype(BF16)
    return jnp.dot(activated, down_w, preferred_element_type=F32)


def core_half(block, rows):
    return lax.dynamic_slice_in_dim(block, (lax.axis_index("tm") % 2) * rows, rows, block.ndim - 2)


def after(value, *earlier):
    return lax.optimization_barrier((value, *earlier))[0]


def body(video, conv_taps, modulation, w_qkv, w_out, w_up, w_down):
    frames_in = video[0]
    tap_set = conv_taps[0]
    mod_table = modulation[0]
    frames, tokens = frames_in.shape[:2]
    n_space = lax.axis_size("space")
    qkv_own = w_qkv[0].transpose(1, 2, 0)
    out_own = w_out[0]
    up_own = w_up[0].T
    down_own = w_down[0]

    half = qkv_own.shape[1] // 2
    place, members = lax.axis_index("tm"), lax.axis_size("tm")
    share = up_own.shape[0] // members

    earlier = shifted(frames_in, "tm", 1)
    near = jnp.concatenate([core_half(qkv_own, half), core_half(out_own, half)[None]], axis=0)
    near = flip(near, "space")
    near_more = flip(near, "tm")
    near = jnp.concatenate([near, near_more], axis=1)
    far = jnp.concatenate(
        [lax.dynamic_slice_in_dim(w, place * share, share, 0) for w in (up_own, down_own)], axis=0
    )
    far = rotate(far, "space", n_space // 2)

    extended = jnp.concatenate([earlier, frames_in], axis=0).astype(F32)
    mixed_rows = (
        extended[2:]
        + tap_set[0] * extended[2:]
        + tap_set[1] * extended[1:-1]
        + tap_set[2] * extended[:-2]
    ).astype(BF16)
    mixed_f32 = mixed_rows.astype(F32)

    attn_in = modulated(mixed_f32, mod_table[0], mod_table[1])
    outgoing = jnp.broadcast_to(attn_in[None], (n_space // frames, frames, tokens, D))
    rows = lax.all_to_all(outgoing.reshape(n_space, tokens, D), "space", 0, 0, tiled=True)
    rows = rows.reshape(n_space * tokens, D)
    attn_part = attend(rows, qkv_own, out_own) + attend(rows, near[:3], near[3])
    attn_part = attn_part.astype(BF16).reshape(n_space, tokens, D)
    far = after(far, attn_part)
    turned = [far]
    for k in range(1, members // 2):
        turned.append(turn_z(far, k))
    far = jnp.stack(turned)
    parts = lax.all_to_all(attn_part, "space", 0, 0, tiled=True)
    attn_sum = jnp.sum(parts.reshape(n_space // frames, frames, tokens, D).astype(F32), axis=0)
    hidden_state = mixed_f32 + mod_table[2] * attn_sum
    mlp_in = modulated(hidden_state, mod_table[3], mod_table[4])
    far_more = flip(far, "tm")
    up_all = jnp.concatenate([up_own] + [w[:, :share].reshape(-1, D) for w in (far, far_more)])
    down_all = jnp.concatenate([down_own] + [w[:, share:].reshape(-1, D) for w in (far, far_more)])

    visits = []
    for frame, way in ((0, 1), (1, -1)):
        visits.append([mlp_in[frame]])
        for move in (way, -way, 2 * way):
            visits[frame].append(rotate(mlp_in[frame], "space", move))
    next_in = []
    for frame, way in ((0, 1), (1, -1)):
        visitors = jnp.stack(visits[frame]).reshape(-1, D)
        part = feed_forward(visitors, up_all, down_all).astype(BF16).reshape(-1, tokens, D)
        total = part[0].astype(F32)
        for k, move in enumerate((way, -way, 2 * way)):
            returned = rotate(part[k + 1], "space", -move)
            if frame:
                returned = after(returned, *next_in)
            total = total + returned.astype(F32)
        next_in.append((hidden_state[frame] + mod_table[5] * total).astype(BF16))
    moved = []
    for frame in range(frames):
        moved.append(rotate(next_in[frame], "section", 1))
    return jnp.stack(moved)[None]


def solution(mesh):
    placed = (
        P("section", "tm", "space", None),
        P("section", None, None),
        P("section", None, None),
        P("section", None, None, "space"),
        P("section", "space", None),
        P("section", None, "space"),
        P("section", "space", None),
    )

    return jax.shard_map(
        body,
        mesh=mesh,
        in_specs=placed,
        out_specs=P("section", "tm", "space", None),
        check_vma=False,
    )
```

```python
import math

import jax
import jax.numpy as jnp
from jax import lax
from jax.sharding import PartitionSpec as P

D = 1152
HEADS = 16
HEAD = D // HEADS
BF16 = jnp.bfloat16
F32 = jnp.float32


def shifted(value, axis, steps):
    count = lax.axis_size(axis)
    initial, last = (max(0, -steps), min(count, count - steps))
    return lax.ppermute(value, axis, [(source, source + steps) for source in range(initial, last)])


def rotate(block, axis, steps):
    count = lax.axis_size(axis)
    return lax.ppermute(block, axis, [(i, (i + steps) % count) for i in range(count)])


def flip(block, axis):
    return lax.ppermute(block, axis, [(i, i ^ 1) for i in range(lax.axis_size(axis))])


def mirrored(block, steps):
    members, count = lax.axis_size("tm"), lax.axis_size("space")
    route = [
        (t * count + y, t * count + (y + (steps if t % 2 == 0 else -steps)) % count)
        for t in range(members)
        for y in range(count)
    ]
    return lax.ppermute(block, ("tm", "space"), route)


def turn_z(block, steps):
    count = lax.axis_size("tm")
    return lax.ppermute(block, "tm", [(i, (i + 2 * steps) % count) for i in range(count)])


def normalize(values_in):
    centre = jnp.mean(values_in, axis=-1, keepdims=True)
    variance = jnp.mean(jnp.square(values_in - centre), axis=-1, keepdims=True)
    return (values_in - centre) * lax.rsqrt(variance + 1e-06)


def modulated(values_in, shift_row, scale_row):
    return (normalize(values_in) * (1.0 + scale_row) + shift_row).astype(BF16)


def attend(rows, qkv, out_w):
    tokens, heads = rows.shape[0], qkv.shape[1] // HEAD
    projected = jnp.einsum("te,cne->tcn", rows, qkv, preferred_element_type=F32).astype(BF16)
    projected = projected.reshape(tokens, 3, heads, HEAD)
    scores = jnp.einsum(
        "qhe,khe->hqk", projected[:, 0], projected[:, 1], preferred_element_type=F32
    ) * (1.0 / math.sqrt(HEAD))
    probs = jax.nn.softmax(scores, axis=-1).astype(BF16)
    heads_out = jnp.einsum("hqk,khe->qhe", probs, projected[:, 2], preferred_element_type=F32)
    heads_out = heads_out.astype(BF16).reshape(tokens, heads * HEAD)
    return jnp.dot(heads_out, out_w, preferred_element_type=F32)


def feed_forward(rows, up_w, down_w):
    activated = jax.nn.gelu(
        jnp.einsum("te,ne->tn", rows, up_w, preferred_element_type=F32), approximate=True
    ).astype(BF16)
    return jnp.dot(activated, down_w, preferred_element_type=F32)


def core_half(block, rows):
    return lax.dynamic_slice_in_dim(block, (lax.axis_index("tm") % 2) * rows, rows, block.ndim - 2)


def after(value, *earlier):
    return lax.optimization_barrier((value, *earlier))[0]


def body(video, conv_taps, modulation, w_qkv, w_out, w_up, w_down):
    frames_in = video[0]
    tap_set = conv_taps[0]
    mod_table = modulation[0]
    frames, tokens = frames_in.shape[:2]
    n_space = lax.axis_size("space")
    qkv_own = w_qkv[0].transpose(1, 2, 0)
    out_own = w_out[0]
    up_own = w_up[0].T
    down_own = w_down[0]

    half = qkv_own.shape[1] // 2
    place, members = lax.axis_index("tm"), lax.axis_size("tm")
    share = up_own.shape[0] // members

    earlier = shifted(frames_in, "tm", 1)
    near = jnp.concatenate([core_half(qkv_own, half), core_half(out_own, half)[None]], axis=0)
    near = flip(near, "space")
    near_more = flip(near, "tm")
    near = jnp.concatenate([near, near_more], axis=1)
    far = jnp.concatenate(
        [lax.dynamic_slice_in_dim(w, place * share, share, 0) for w in (up_own, down_own)], axis=0
    )
    for _ in range(2):
        far = mirrored(far, n_space // 4)

    extended = jnp.concatenate([earlier, frames_in], axis=0).astype(F32)
    mixed_rows = (
        extended[2:]
        + tap_set[0] * extended[2:]
        + tap_set[1] * extended[1:-1]
        + tap_set[2] * extended[:-2]
    ).astype(BF16)
    mixed_f32 = mixed_rows.astype(F32)

    attn_in = modulated(mixed_f32, mod_table[0], mod_table[1])
    outgoing = jnp.broadcast_to(attn_in[None], (n_space // frames, frames, tokens, D))
    rows = lax.all_to_all(outgoing.reshape(n_space, tokens, D), "space", 0, 0, tiled=True)
    rows = rows.reshape(n_space * tokens, D)
    attn_part = attend(rows, qkv_own, out_own) + attend(rows, near[:3], near[3])
    attn_part = attn_part.astype(BF16).reshape(n_space, tokens, D)
    far = after(far, attn_part)
    turned = [far]
    for k in range(1, members // 2):
        turned.append(turn_z(far, k))
    far = jnp.stack(turned)
    parts = lax.all_to_all(attn_part, "space", 0, 0, tiled=True)
    attn_sum = jnp.sum(parts.reshape(n_space // frames, frames, tokens, D).astype(F32), axis=0)
    hidden_state = mixed_f32 + mod_table[2] * attn_sum
    mlp_in = modulated(hidden_state, mod_table[3], mod_table[4])
    far_more = flip(far, "tm")
    up_all = jnp.concatenate([up_own] + [w[:, :share].reshape(-1, D) for w in (far, far_more)])
    down_all = jnp.concatenate([down_own] + [w[:, share:].reshape(-1, D) for w in (far, far_more)])

    moves = (2, 1, -1)
    visits = [mlp_in]
    for move in moves:
        visits.append(mirrored(mlp_in, move))
    next_in = []
    for frame in range(frames):
        visitors = jnp.stack([visit[frame] for visit in visits]).reshape(-1, D)
        part = feed_forward(visitors, up_all, down_all).astype(BF16).reshape(-1, tokens, D)
        total = part[0].astype(F32)
        for k, move in enumerate(moves):
            returned = mirrored(part[k + 1], -move)
            if frame:
                returned = after(returned, *next_in)
            total = total + returned.astype(F32)
        next_in.append((hidden_state[frame] + mod_table[5] * total).astype(BF16))

    sections = lax.axis_size("section")
    crossed = lax.ppermute(
        next_in[0], "section", [(s, (s + 4) % sections) for s in range(3, sections, 4)]
    )
    second = rotate(next_in[1], "section", 1)
    first = jnp.where(lax.axis_index("section") % 4 == 3, crossed, next_in[0])
    first = lax.ppermute(first, "section", [(s, s // 4 * 4 + (s + 1) % 4) for s in range(sections)])
    return jnp.stack([first, second])[None]


def solution(mesh):
    placed = (
        P("section", "tm", "space", None),
        P("section", None, None),
        P("section", None, None),
        P("section", None, None, "space"),
        P("section", "space", None),
        P("section", None, "space"),
        P("section", "space", None),
    )

    return jax.shard_map(
        body,
        mesh=mesh,
        in_specs=placed,
        out_specs=P("section", "tm", "space", None),
        check_vma=False,
    )
```

```python
import math

import jax
import jax.numpy as jnp
from jax import lax
from jax.sharding import PartitionSpec as P

D = 1152
HEADS = 16
HEAD = D // HEADS
BF16 = jnp.bfloat16
F32 = jnp.float32


def shifted(value, axis, steps):
    count = lax.axis_size(axis)
    initial, last = (max(0, -steps), min(count, count - steps))
    return lax.ppermute(value, axis, [(source, source + steps) for source in range(initial, last)])


def rotate(block, axis, steps):
    count = lax.axis_size(axis)
    return lax.ppermute(block, axis, [(i, (i + steps) % count) for i in range(count)])


def flip(block, axis):
    return lax.ppermute(block, axis, [(i, i ^ 1) for i in range(lax.axis_size(axis))])


def mirrored(block, steps):
    members, count = lax.axis_size("tm"), lax.axis_size("space")
    route = [
        (t * count + y, t * count + (y + (steps if t % 2 == 0 else -steps)) % count)
        for t in range(members)
        for y in range(count)
    ]
    return lax.ppermute(block, ("tm", "space"), route)


def turn_z(block, steps):
    count = lax.axis_size("tm")
    return lax.ppermute(block, "tm", [(i, (i + 2 * steps) % count) for i in range(count)])


def normalize(values_in):
    centre = jnp.mean(values_in, axis=-1, keepdims=True)
    variance = jnp.mean(jnp.square(values_in - centre), axis=-1, keepdims=True)
    return (values_in - centre) * lax.rsqrt(variance + 1e-06)


def modulated(values_in, shift_row, scale_row):
    return (normalize(values_in) * (1.0 + scale_row) + shift_row).astype(BF16)


def attend(rows, qkv, out_w):
    tokens, heads = rows.shape[0], qkv.shape[1] // HEAD
    projected = jnp.einsum("te,cne->tcn", rows, qkv, preferred_element_type=F32).astype(BF16)
    projected = projected.reshape(tokens, 3, heads, HEAD)
    scores = jnp.einsum(
        "qhe,khe->hqk", projected[:, 0], projected[:, 1], preferred_element_type=F32
    ) * (1.0 / math.sqrt(HEAD))
    probs = jax.nn.softmax(scores, axis=-1).astype(BF16)
    heads_out = jnp.einsum("hqk,khe->qhe", probs, projected[:, 2], preferred_element_type=F32)
    heads_out = heads_out.astype(BF16).reshape(tokens, heads * HEAD)
    return jnp.dot(heads_out, out_w, preferred_element_type=F32)


def feed_forward(rows, up_w, down_w):
    activated = jax.nn.gelu(
        jnp.einsum("te,ne->tn", rows, up_w, preferred_element_type=F32), approximate=True
    ).astype(BF16)
    return jnp.dot(activated, down_w, preferred_element_type=F32)


def core_half(block, rows):
    return lax.dynamic_slice_in_dim(block, (lax.axis_index("tm") % 2) * rows, rows, block.ndim - 2)


def after(value, *earlier):
    return lax.optimization_barrier((value, *earlier))[0]


def body(video, conv_taps, modulation, w_qkv, w_out, w_up, w_down):
    frames_in = video[0]
    tap_set = conv_taps[0]
    mod_table = modulation[0]
    frames, tokens = frames_in.shape[:2]
    n_space = lax.axis_size("space")
    qkv_own = w_qkv[0].transpose(1, 2, 0)
    out_own = w_out[0]
    up_own = w_up[0].T
    down_own = w_down[0]

    half = qkv_own.shape[1] // 2
    place, members = lax.axis_index("tm"), lax.axis_size("tm")
    share = up_own.shape[0] // members

    earlier = shifted(frames_in, "tm", 1)
    near = jnp.concatenate([core_half(qkv_own, half), core_half(out_own, half)[None]], axis=0)
    near = flip(near, "space")
    near_more = flip(near, "tm")
    near = jnp.concatenate([near, near_more], axis=1)
    far = jnp.concatenate(
        [lax.dynamic_slice_in_dim(w, place * share, share, 0) for w in (up_own, down_own)], axis=0
    )
    far = rotate(far, "space", n_space // 2)

    extended = jnp.concatenate([earlier, frames_in], axis=0).astype(F32)
    mixed_rows = (
        extended[2:]
        + tap_set[0] * extended[2:]
        + tap_set[1] * extended[1:-1]
        + tap_set[2] * extended[:-2]
    ).astype(BF16)
    mixed_f32 = mixed_rows.astype(F32)

    attn_in = modulated(mixed_f32, mod_table[0], mod_table[1])
    outgoing = jnp.broadcast_to(attn_in[None], (n_space // frames, frames, tokens, D))
    rows = lax.all_to_all(outgoing.reshape(n_space, tokens, D), "space", 0, 0, tiled=True)
    rows = rows.reshape(n_space * tokens, D)
    attn_part = attend(rows, qkv_own, out_own) + attend(rows, near[:3], near[3])
    attn_part = attn_part.astype(BF16).reshape(n_space, tokens, D)
    far = after(far, attn_part)
    turned = [far]
    for k in range(1, members // 2):
        turned.append(turn_z(far, k))
    far = jnp.stack(turned)
    parts = lax.all_to_all(attn_part, "space", 0, 0, tiled=True)
    attn_sum = jnp.sum(parts.reshape(n_space // frames, frames, tokens, D).astype(F32), axis=0)
    hidden_state = mixed_f32 + mod_table[2] * attn_sum
    mlp_in = modulated(hidden_state, mod_table[3], mod_table[4])
    far_more = flip(far, "tm")
    up_all = jnp.concatenate([up_own] + [w[:, :share].reshape(-1, D) for w in (far, far_more)])
    down_all = jnp.concatenate([down_own] + [w[:, share:].reshape(-1, D) for w in (far, far_more)])

    moves = (2, 1, -1)
    visits = [mlp_in]
    for move in moves:
        visits.append(mirrored(mlp_in, move))
    next_in = []
    for frame in range(frames):
        visitors = jnp.stack([visit[frame] for visit in visits]).reshape(-1, D)
        part = feed_forward(visitors, up_all, down_all).astype(BF16).reshape(-1, tokens, D)
        total = part[0].astype(F32)
        for k, move in enumerate(moves):
            returned = mirrored(part[k + 1], -move)
            if frame:
                returned = after(returned, *next_in)
            total = total + returned.astype(F32)
        next_in.append((hidden_state[frame] + mod_table[5] * total).astype(BF16))

    sections = lax.axis_size("section")
    at_end = lax.axis_index("section") % 4 == 3
    handed = []
    for frame in range(frames):
        crossed = lax.ppermute(
            next_in[frame], "section", [(s, (s + 4) % sections) for s in range(3, sections, 4)]
        )
        leaving = jnp.where(at_end, crossed, next_in[frame])
        handed.append(
            lax.ppermute(
                leaving, "section", [(s, s // 4 * 4 + (s + 1) % 4) for s in range(sections)]
            )
        )
    return jnp.stack(handed)[None]


def solution(mesh):
    placed = (
        P("section", "tm", "space", None),
        P("section", None, None),
        P("section", None, None),
        P("section", None, None, "space"),
        P("section", "space", None),
        P("section", None, "space"),
        P("section", "space", None),
    )

    return jax.shard_map(
        body,
        mesh=mesh,
        in_specs=placed,
        out_specs=P("section", "tm", "space", None),
        check_vma=False,
    )
```

```python
import math

import jax
import jax.numpy as jnp
from jax import lax
from jax.sharding import PartitionSpec as P

D = 1152
HEADS = 16
HEAD = D // HEADS
BF16 = jnp.bfloat16
F32 = jnp.float32


def shifted(value, axis, steps):
    count = lax.axis_size(axis)
    initial, last = (max(0, -steps), min(count, count - steps))
    return lax.ppermute(value, axis, [(source, source + steps) for source in range(initial, last)])


def rotate(block, axis, steps):
    count = lax.axis_size(axis)
    return lax.ppermute(block, axis, [(i, (i + steps) % count) for i in range(count)])


def flip(block, axis):
    return lax.ppermute(block, axis, [(i, i ^ 1) for i in range(lax.axis_size(axis))])


def mirrored(block, steps):
    members, count = lax.axis_size("tm"), lax.axis_size("space")
    route = [
        (t * count + y, t * count + (y + (steps if t % 2 == 0 else -steps)) % count)
        for t in range(members)
        for y in range(count)
    ]
    return lax.ppermute(block, ("tm", "space"), route)


def turn_z(block, steps):
    count = lax.axis_size("tm")
    return lax.ppermute(block, "tm", [(i, (i + 2 * steps) % count) for i in range(count)])


def normalize(values_in):
    centre = jnp.mean(values_in, axis=-1, keepdims=True)
    variance = jnp.mean(jnp.square(values_in - centre), axis=-1, keepdims=True)
    return (values_in - centre) * lax.rsqrt(variance + 1e-06)


def modulated(values_in, shift_row, scale_row):
    return (normalize(values_in) * (1.0 + scale_row) + shift_row).astype(BF16)


def attend(rows, qkv, out_w):
    tokens, heads = rows.shape[0], qkv.shape[1] // HEAD
    projected = jnp.einsum("te,cne->tcn", rows, qkv, preferred_element_type=F32).astype(BF16)
    projected = projected.reshape(tokens, 3, heads, HEAD)
    scores = jnp.einsum(
        "qhe,khe->hqk", projected[:, 0], projected[:, 1], preferred_element_type=F32
    ) * (1.0 / math.sqrt(HEAD))
    probs = jax.nn.softmax(scores, axis=-1).astype(BF16)
    heads_out = jnp.einsum("hqk,khe->qhe", probs, projected[:, 2], preferred_element_type=F32)
    heads_out = heads_out.astype(BF16).reshape(tokens, heads * HEAD)
    return jnp.dot(heads_out, out_w, preferred_element_type=F32)


def feed_forward(rows, up_w, down_w):
    activated = jax.nn.gelu(
        jnp.einsum("te,ne->tn", rows, up_w, preferred_element_type=F32), approximate=True
    ).astype(BF16)
    return jnp.dot(activated, down_w, preferred_element_type=F32)


def core_half(block, rows):
    return lax.dynamic_slice_in_dim(block, (lax.axis_index("tm") % 2) * rows, rows, block.ndim - 2)


def after(value, *earlier):
    return lax.optimization_barrier((value, *earlier))[0]


def body(video, conv_taps, modulation, w_qkv, w_out, w_up, w_down):
    frames_in = video[0]
    tap_set = conv_taps[0]
    mod_table = modulation[0]
    frames, tokens = frames_in.shape[:2]
    n_space = lax.axis_size("space")
    qkv_own = w_qkv[0].transpose(1, 2, 0)
    out_own = w_out[0]
    up_own = w_up[0].T
    down_own = w_down[0]

    half = qkv_own.shape[1] // 2
    place, members = lax.axis_index("tm"), lax.axis_size("tm")
    share = up_own.shape[0] // members

    earlier = shifted(frames_in, "tm", 1)
    near = jnp.concatenate([core_half(qkv_own, half), core_half(out_own, half)[None]], axis=0)
    near = flip(near, "space")
    near_more = flip(near, "tm")
    near = jnp.concatenate([near, near_more], axis=1)
    far = jnp.concatenate(
        [lax.dynamic_slice_in_dim(w, place * share, share, 0) for w in (up_own, down_own)], axis=0
    )
    far = rotate(far, "space", n_space // 2)

    extended = jnp.concatenate([earlier, frames_in], axis=0).astype(F32)
    mixed_rows = (
        extended[2:]
        + tap_set[0] * extended[2:]
        + tap_set[1] * extended[1:-1]
        + tap_set[2] * extended[:-2]
    ).astype(BF16)
    mixed_f32 = mixed_rows.astype(F32)

    attn_in = modulated(mixed_f32, mod_table[0], mod_table[1])
    outgoing = jnp.broadcast_to(attn_in[None], (n_space // frames, frames, tokens, D))
    rows = lax.all_to_all(outgoing.reshape(n_space, tokens, D), "space", 0, 0, tiled=True)
    rows = rows.reshape(n_space * tokens, D)
    attn_part = attend(rows, qkv_own, out_own) + attend(rows, near[:3], near[3])
    attn_part = attn_part.astype(BF16).reshape(n_space, tokens, D)
    far = after(far, attn_part)
    turned = [far]
    for k in range(1, members // 2):
        turned.append(turn_z(far, k))
    far = jnp.stack(turned)
    parts = lax.all_to_all(attn_part, "space", 0, 0, tiled=True)
    attn_sum = jnp.sum(parts.reshape(n_space // frames, frames, tokens, D).astype(F32), axis=0)
    hidden_state = mixed_f32 + mod_table[2] * attn_sum
    mlp_in = modulated(hidden_state, mod_table[3], mod_table[4])
    far_more = flip(far, "tm")
    up_all = jnp.concatenate([up_own] + [w[:, :share].reshape(-1, D) for w in (far, far_more)])
    down_all = jnp.concatenate([down_own] + [w[:, share:].reshape(-1, D) for w in (far, far_more)])

    moves = (2, 1, -1)
    visits = [mlp_in]
    for move in moves:
        visits.append(mirrored(mlp_in, move))
    part = feed_forward(jnp.stack(visits).reshape(-1, D), up_all, down_all)
    part = part.astype(BF16).reshape(-1, frames, tokens, D)
    mlp_sum = part[0].astype(F32)
    for k, move in enumerate(moves):
        mlp_sum = mlp_sum + mirrored(part[k + 1], -move).astype(F32)
    layer_out = (hidden_state + mod_table[5] * mlp_sum).astype(BF16)

    sections = lax.axis_size("section")
    place_x = lax.axis_index("section") % 4
    along_x = [(s, s // 4 * 4 + (s + 1) % 4) for s in range(sections)]

    def crossing(block, x):
        return lax.ppermute(block, "section", [(s, (s + 4) % sections) for s in range(x, sections, 4)])

    second = lax.ppermute(layer_out[1], "section", along_x)
    crossed = crossing(layer_out[0], 3)
    first = jnp.where(place_x == 3, crossed, layer_out[0])
    first = lax.ppermute(first, "section", along_x)
    crossed = crossing(second, 0)
    second = jnp.where(place_x == 0, crossed, second)
    return jnp.stack([first, second])[None]


def solution(mesh):
    placed = (
        P("section", "tm", "space", None),
        P("section", None, None),
        P("section", None, None),
        P("section", None, None, "space"),
        P("section", "space", None),
        P("section", None, "space"),
        P("section", "space", None),
    )

    return jax.shard_map(
        body,
        mesh=mesh,
        in_specs=placed,
        out_specs=P("section", "tm", "space", None),
        check_vma=False,
    )
```

```python
import math

import jax
import jax.numpy as jnp
from jax import lax
from jax.experimental import pallas as pl
from jax.experimental.pallas import tpu as pltpu
from jax.sharding import PartitionSpec as P

D = 1152
HEADS = 16
HEAD = D // HEADS
BF16 = jnp.bfloat16
F32 = jnp.float32


def shifted(value, axis, steps):
    count = lax.axis_size(axis)
    initial, last = (max(0, -steps), min(count, count - steps))
    return lax.ppermute(value, axis, [(source, source + steps) for source in range(initial, last)])


def rotate(block, axis, steps):
    count = lax.axis_size(axis)
    return lax.ppermute(block, axis, [(i, (i + steps) % count) for i in range(count)])


def flip(block, axis):
    return lax.ppermute(block, axis, [(i, i ^ 1) for i in range(lax.axis_size(axis))])


def mirrored(block, steps):
    members, count = lax.axis_size("tm"), lax.axis_size("space")
    route = [
        (t * count + y, t * count + (y + (steps if t % 2 == 0 else -steps)) % count)
        for t in range(members)
        for y in range(count)
    ]
    return lax.ppermute(block, ("tm", "space"), route)


def turn_z(block, steps):
    count = lax.axis_size("tm")
    return lax.ppermute(block, "tm", [(i, (i + 2 * steps) % count) for i in range(count)])


def normalize(values_in):
    centre = jnp.mean(values_in, axis=-1, keepdims=True)
    variance = jnp.mean(jnp.square(values_in - centre), axis=-1, keepdims=True)
    return (values_in - centre) * lax.rsqrt(variance + 1e-06)


def modulated(values_in, shift_row, scale_row):
    return (normalize(values_in) * (1.0 + scale_row) + shift_row).astype(BF16)


def attention_kernel(rows_ref, own_ref, own_out_ref, near_ref, part_ref, heads_ref):
    rows = rows_ref[...]
    columns = own_out_ref.shape[0]
    total = None
    for side in range(2):
        qkv_w = own_ref[...] if side == 0 else near_ref[: 3 * columns]
        out_w = own_out_ref[...] if side == 0 else near_ref[3 * columns :]
        projected = lax.dot_general(
            qkv_w, rows, (((1,), (1,)), ((), ())), preferred_element_type=F32
        )
        for head in range(columns // HEAD):
            q, k, v = (
                projected[c * columns + head * HEAD : c * columns + (head + 1) * HEAD].astype(BF16)
                for c in range(3)
            )
            scores = lax.dot_general(k, q, (((0,), (0,)), ((), ())), preferred_element_type=F32)
            top = jnp.max(scores, axis=0, keepdims=True)
            weight = jnp.exp((scores - top) * (1.0 / math.sqrt(HEAD)))
            mass = jnp.sum(weight, axis=0, keepdims=True)
            mixed = jnp.dot(v, weight.astype(BF16), preferred_element_type=F32)
            heads_ref[head * HEAD : (head + 1) * HEAD] = mixed / mass
        part = lax.dot_general(
            heads_ref[...].astype(BF16), out_w, (((0,), (0,)), ((), ())), preferred_element_type=F32
        )
        total = part if total is None else total + part
    part_ref[...] = total.astype(BF16)


def attend(rows, qkv_own, out_own, near):
    tokens, columns = rows.shape[0], out_own.shape[0]
    return pl.pallas_call(
        attention_kernel,
        out_shape=jax.ShapeDtypeStruct((tokens, D), BF16),
        scratch_shapes=[pltpu.VMEM((columns, tokens), F32)],
        name="frame_attention",
    )(rows, qkv_own, out_own, near)


def feed_forward(rows, up_w, down_w):
    activated = jax.nn.gelu(
        jnp.einsum("te,ne->tn", rows, up_w, preferred_element_type=F32), approximate=True
    ).astype(BF16)
    return jnp.dot(activated, down_w, preferred_element_type=F32)


def core_half(block, rows):
    return lax.dynamic_slice_in_dim(block, (lax.axis_index("tm") % 2) * rows, rows, block.ndim - 2)


def after(value, *earlier):
    return lax.optimization_barrier((value, *earlier))[0]


def body(video, conv_taps, modulation, w_qkv, w_out, w_up, w_down):
    frames_in = video[0]
    tap_set = conv_taps[0]
    mod_table = modulation[0]
    frames, tokens = frames_in.shape[:2]
    n_space = lax.axis_size("space")
    qkv_own = w_qkv[0].transpose(1, 2, 0)
    out_own = w_out[0]
    up_own = w_up[0].T
    down_own = w_down[0]

    half = qkv_own.shape[1] // 2
    place, members = lax.axis_index("tm"), lax.axis_size("tm")
    share = up_own.shape[0] // members

    earlier = shifted(frames_in, "tm", 1)
    near = jnp.concatenate([core_half(qkv_own, half), core_half(out_own, half)[None]], axis=0)
    near = flip(near, "space")
    near_more = flip(near, "tm")
    near = jnp.concatenate([near, near_more], axis=1)
    far = jnp.concatenate(
        [lax.dynamic_slice_in_dim(w, place * share, share, 0) for w in (up_own, down_own)], axis=0
    )
    far = rotate(far, "space", n_space // 2)

    extended = jnp.concatenate([earlier, frames_in], axis=0).astype(F32)
    mixed_rows = (
        extended[2:]
        + tap_set[0] * extended[2:]
        + tap_set[1] * extended[1:-1]
        + tap_set[2] * extended[:-2]
    ).astype(BF16)
    mixed_f32 = mixed_rows.astype(F32)

    attn_in = modulated(mixed_f32, mod_table[0], mod_table[1])
    outgoing = jnp.broadcast_to(attn_in[None], (n_space // frames, frames, tokens, D))
    rows = lax.all_to_all(outgoing.reshape(n_space, tokens, D), "space", 0, 0, tiled=True)
    rows = rows.reshape(n_space * tokens, D)
    attn_part = attend(rows, qkv_own.reshape(-1, D), out_own, near.reshape(-1, D))
    attn_part = attn_part.reshape(n_space, tokens, D)
    far = after(far, attn_part)
    turned = [far]
    for k in range(1, members // 2):
        turned.append(turn_z(far, k))
    far = jnp.stack(turned)
    parts = lax.all_to_all(attn_part, "space", 0, 0, tiled=True)
    attn_sum = jnp.sum(parts.reshape(n_space // frames, frames, tokens, D).astype(F32), axis=0)
    hidden_state = mixed_f32 + mod_table[2] * attn_sum
    mlp_in = modulated(hidden_state, mod_table[3], mod_table[4])
    far_more = flip(far, "tm")
    up_all = jnp.concatenate([up_own] + [w[:, :share].reshape(-1, D) for w in (far, far_more)])
    down_all = jnp.concatenate([down_own] + [w[:, share:].reshape(-1, D) for w in (far, far_more)])

    moves = (2, 1, -1)
    visits = [mlp_in]
    for move in moves:
        visits.append(mirrored(mlp_in, move))
    part = feed_forward(jnp.stack(visits).reshape(-1, D), up_all, down_all)
    part = part.astype(BF16).reshape(-1, frames, tokens, D)
    mlp_sum = part[0].astype(F32)
    for k, move in enumerate(moves):
        mlp_sum = mlp_sum + mirrored(part[k + 1], -move).astype(F32)
    layer_out = (hidden_state + mod_table[5] * mlp_sum).astype(BF16)

    sections = lax.axis_size("section")
    place_x = lax.axis_index("section") % 4
    along_x = [(s, s // 4 * 4 + (s + 1) % 4) for s in range(sections)]

    def crossing(block, x):
        return lax.ppermute(block, "section", [(s, (s + 4) % sections) for s in range(x, sections, 4)])

    second = lax.ppermute(layer_out[1], "section", along_x)
    crossed = crossing(layer_out[0], 3)
    first = jnp.where(place_x == 3, crossed, layer_out[0])
    first = lax.ppermute(first, "section", along_x)
    crossed = crossing(second, 0)
    second = jnp.where(place_x == 0, crossed, second)
    return jnp.stack([first, second])[None]


def solution(mesh):
    placed = (
        P("section", "tm", "space", None),
        P("section", None, None),
        P("section", None, None),
        P("section", None, None, "space"),
        P("section", "space", None),
        P("section", None, "space"),
        P("section", "space", None),
    )

    return jax.shard_map(
        body,
        mesh=mesh,
        in_specs=placed,
        out_specs=P("section", "tm", "space", None),
        check_vma=False,
    )
```

```python
import math

import jax
import jax.numpy as jnp
from jax import lax
from jax.experimental import pallas as pl
from jax.experimental.pallas import tpu as pltpu
from jax.sharding import PartitionSpec as P

D = 1152
HEADS = 16
HEAD = D // HEADS
BF16 = jnp.bfloat16
F32 = jnp.float32


def shifted(value, axis, steps):
    count = lax.axis_size(axis)
    initial, last = (max(0, -steps), min(count, count - steps))
    return lax.ppermute(value, axis, [(source, source + steps) for source in range(initial, last)])


def rotate(block, axis, steps):
    count = lax.axis_size(axis)
    return lax.ppermute(block, axis, [(i, (i + steps) % count) for i in range(count)])


def flip(block, axis):
    return lax.ppermute(block, axis, [(i, i ^ 1) for i in range(lax.axis_size(axis))])


def mirrored(block, steps):
    members, count = lax.axis_size("tm"), lax.axis_size("space")
    route = [
        (t * count + y, t * count + (y + (steps if t % 2 == 0 else -steps)) % count)
        for t in range(members)
        for y in range(count)
    ]
    return lax.ppermute(block, ("tm", "space"), route)


def turn_z(block, steps):
    count = lax.axis_size("tm")
    return lax.ppermute(block, "tm", [(i, (i + 2 * steps) % count) for i in range(count)])


def normalize(values_in):
    centre = jnp.mean(values_in, axis=-1, keepdims=True)
    variance = jnp.mean(jnp.square(values_in - centre), axis=-1, keepdims=True)
    return (values_in - centre) * lax.rsqrt(variance + 1e-06)


def modulated(values_in, shift_row, scale_row):
    return (normalize(values_in) * (1.0 + scale_row) + shift_row).astype(BF16)


def attention_kernel(rows_ref, own_ref, own_out_ref, near_ref, part_ref, heads_ref):
    rows = rows_ref[...]
    columns = own_out_ref.shape[0]
    total = None
    for side in range(2):
        qkv_w = own_ref[...] if side == 0 else near_ref[: 3 * columns]
        out_w = own_out_ref[...] if side == 0 else near_ref[3 * columns :]
        projected = lax.dot_general(
            qkv_w, rows, (((1,), (1,)), ((), ())), preferred_element_type=F32
        )
        for head in range(columns // HEAD):
            q, k, v = (
                projected[c * columns + head * HEAD : c * columns + (head + 1) * HEAD].astype(BF16)
                for c in range(3)
            )
            scores = lax.dot_general(k, q, (((0,), (0,)), ((), ())), preferred_element_type=F32)
            top = jnp.max(scores, axis=0, keepdims=True)
            weight = jnp.exp((scores - top) * (1.0 / math.sqrt(HEAD)))
            mass = jnp.sum(weight, axis=0, keepdims=True)
            mixed = jnp.dot(v, weight.astype(BF16), preferred_element_type=F32)
            heads_ref[head * HEAD : (head + 1) * HEAD] = mixed / mass
        part = lax.dot_general(
            heads_ref[...].astype(BF16), out_w, (((0,), (0,)), ((), ())), preferred_element_type=F32
        )
        total = part if total is None else total + part
    part_ref[...] = total.astype(BF16)


def attend(rows, qkv_own, out_own, near):
    tokens, columns = rows.shape[0], out_own.shape[0]
    return pl.pallas_call(
        attention_kernel,
        out_shape=jax.ShapeDtypeStruct((tokens, D), BF16),
        scratch_shapes=[pltpu.VMEM((columns, tokens), F32)],
        name="frame_attention",
    )(rows, qkv_own, out_own, near)


def feed_forward(rows, up_w, down_w):
    activated = jax.nn.gelu(
        jnp.einsum("te,ne->tn", rows, up_w, preferred_element_type=F32), approximate=True
    ).astype(BF16)
    return jnp.dot(activated, down_w, preferred_element_type=F32)


def core_half(block, rows):
    return lax.dynamic_slice_in_dim(block, (lax.axis_index("tm") % 2) * rows, rows, block.ndim - 2)


def after(value, *earlier):
    return lax.optimization_barrier((value, *earlier))[0]


def body(video, conv_taps, modulation, w_qkv, w_out, w_up, w_down):
    frames_in = video[0]
    tap_set = conv_taps[0]
    mod_table = modulation[0]
    frames, tokens = frames_in.shape[:2]
    n_space = lax.axis_size("space")
    qkv_own = w_qkv[0].transpose(1, 2, 0)
    out_own = w_out[0]
    up_own = w_up[0].T
    down_own = w_down[0]

    half = qkv_own.shape[1] // 2
    place, members = lax.axis_index("tm"), lax.axis_size("tm")
    share = up_own.shape[0] // members

    earlier = shifted(frames_in, "tm", 1)
    near = jnp.concatenate([core_half(qkv_own, half), core_half(out_own, half)[None]], axis=0)
    near = flip(near, "space")
    near_more = flip(near, "tm")
    near = jnp.concatenate([near, near_more], axis=1)
    far = jnp.concatenate(
        [lax.dynamic_slice_in_dim(w, place * share, share, 0) for w in (up_own, down_own)], axis=0
    )
    far = rotate(far, "space", n_space // 2)

    extended = jnp.concatenate([earlier, frames_in], axis=0).astype(F32)
    mixed_rows = (
        extended[2:]
        + tap_set[0] * extended[2:]
        + tap_set[1] * extended[1:-1]
        + tap_set[2] * extended[:-2]
    ).astype(BF16)
    mixed_f32 = mixed_rows.astype(F32)

    attn_in = modulated(mixed_f32, mod_table[0], mod_table[1])
    outgoing = jnp.broadcast_to(attn_in[None], (n_space // frames, frames, tokens, D))
    rows = lax.all_to_all(outgoing.reshape(n_space, tokens, D), "space", 0, 0, tiled=True)
    rows = rows.reshape(n_space * tokens, D)
    attn_part = attend(rows, qkv_own.reshape(-1, D), out_own, near.reshape(-1, D))
    attn_part = attn_part.reshape(n_space, tokens, D)
    far = after(far, attn_part)
    turned = [far]
    for k in range(1, members // 2):
        turned.append(turn_z(far, k))
    far = jnp.stack(turned)
    parts = lax.all_to_all(attn_part, "space", 0, 0, tiled=True)
    attn_sum = jnp.sum(parts.reshape(n_space // frames, frames, tokens, D).astype(F32), axis=0)
    hidden_state = mixed_f32 + mod_table[2] * attn_sum
    mlp_in = modulated(hidden_state, mod_table[3], mod_table[4])
    far_more = flip(far, "tm")
    up_all = jnp.concatenate([up_own] + [w[:, :share].reshape(-1, D) for w in (far, far_more)])
    down_all = jnp.concatenate([down_own] + [w[:, share:].reshape(-1, D) for w in (far, far_more)])

    moves = (2, 1, -1)
    visits = [mlp_in]
    for move in moves:
        visits.append(mirrored(mlp_in, move))
    part = feed_forward(jnp.stack(visits).reshape(-1, D), up_all, down_all)
    part = part.astype(BF16).reshape(-1, frames, tokens, D)
    mlp_sum = part[0].astype(F32)
    for k, move in enumerate(moves):
        mlp_sum = mlp_sum + mirrored(part[k + 1], -move).astype(F32)
    layer_out = (hidden_state + mod_table[5] * mlp_sum).astype(BF16)

    sections = lax.axis_size("section")
    place_x = lax.axis_index("section") % 4
    along_x = [(s, s // 4 * 4 + (s + 1) % 4) for s in range(sections)]

    def crossing(block, x):
        return lax.ppermute(block, "section", [(s, (s + 4) % sections) for s in range(x, sections, 4)])

    second = lax.ppermute(layer_out[1], "section", along_x)
    crossed = crossing(layer_out[0], 3)
    first = lax.ppermute(layer_out[0], "section", [(s, d) for s, d in along_x if d == s + 1])
    crossed_second = crossing(second, 0)
    first_end = lax.ppermute(crossed, "section", [(s, d) for s, d in along_x if d != s + 1])
    arrived = [jnp.where(place_x == 0, first_end, first), jnp.where(place_x == 0, crossed_second, second)]
    return jnp.stack(arrived)[None]


def solution(mesh):
    placed = (
        P("section", "tm", "space", None),
        P("section", None, None),
        P("section", None, None),
        P("section", None, None, "space"),
        P("section", "space", None),
        P("section", None, "space"),
        P("section", "space", None),
    )

    return jax.shard_map(
        body,
        mesh=mesh,
        in_specs=placed,
        out_specs=P("section", "tm", "space", None),
        check_vma=False,
    )
```

```python
import math

import jax
import jax.numpy as jnp
from jax import lax
from jax.experimental import pallas as pl
from jax.experimental.pallas import tpu as pltpu
from jax.sharding import PartitionSpec as P

D = 1152
HEADS = 16
HEAD = D // HEADS
BF16 = jnp.bfloat16
F32 = jnp.float32


def shifted(value, axis, steps):
    count = lax.axis_size(axis)
    initial, last = (max(0, -steps), min(count, count - steps))
    return lax.ppermute(value, axis, [(source, source + steps) for source in range(initial, last)])


def rotate(block, axis, steps):
    count = lax.axis_size(axis)
    return lax.ppermute(block, axis, [(i, (i + steps) % count) for i in range(count)])


def flip(block, axis):
    return lax.ppermute(block, axis, [(i, i ^ 1) for i in range(lax.axis_size(axis))])


def mirrored(block, steps):
    members, count = lax.axis_size("tm"), lax.axis_size("space")
    route = [
        (t * count + y, t * count + (y + (steps if t % 2 == 0 else -steps)) % count)
        for t in range(members)
        for y in range(count)
    ]
    return lax.ppermute(block, ("tm", "space"), route)


def turn_z(block, steps):
    count = lax.axis_size("tm")
    return lax.ppermute(block, "tm", [(i, (i + 2 * steps) % count) for i in range(count)])


def normalize(values_in):
    centre = jnp.mean(values_in, axis=-1, keepdims=True)
    variance = jnp.mean(jnp.square(values_in - centre), axis=-1, keepdims=True)
    return (values_in - centre) * lax.rsqrt(variance + 1e-06)


def modulated(values_in, shift_row, scale_row):
    return (normalize(values_in) * (1.0 + scale_row) + shift_row).astype(BF16)


def attention_kernel(rows_ref, own_ref, near_ref, own_heads_ref, near_heads_ref, heads_ref):
    rows = rows_ref[...]
    columns = own_ref.shape[0] // 3
    for qkv_ref, out_ref in ((own_ref, own_heads_ref), (near_ref, near_heads_ref)):
        projected = lax.dot_general(
            qkv_ref[...], rows, (((1,), (1,)), ((), ())), preferred_element_type=F32
        )
        for head in range(columns // HEAD):
            q, k, v = (
                projected[c * columns + head * HEAD : c * columns + (head + 1) * HEAD].astype(BF16)
                for c in range(3)
            )
            scores = lax.dot_general(k, q, (((0,), (0,)), ((), ())), preferred_element_type=F32)
            top = jnp.max(scores, axis=0, keepdims=True)
            weight = jnp.exp((scores - top) * (1.0 / math.sqrt(HEAD)))
            mass = jnp.sum(weight, axis=0, keepdims=True)
            mixed = jnp.dot(v, weight.astype(BF16), preferred_element_type=F32)
            heads_ref[head * HEAD : (head + 1) * HEAD] = mixed / mass
        out_ref[...] = heads_ref[...].T.astype(BF16)


def attend(rows, qkv_own, qkv_near):
    tokens, columns = rows.shape[0], qkv_own.shape[0] // 3
    return pl.pallas_call(
        attention_kernel,
        out_shape=[jax.ShapeDtypeStruct((tokens, columns), BF16)] * 2,
        scratch_shapes=[pltpu.VMEM((columns, tokens), F32)],
        name="frame_attention",
    )(rows, qkv_own, qkv_near)


def feed_forward(rows, up_w, down_w):
    activated = jax.nn.gelu(
        jnp.einsum("te,ne->tn", rows, up_w, preferred_element_type=F32), approximate=True
    ).astype(BF16)
    return jnp.dot(activated, down_w, preferred_element_type=F32)


def core_half(block, rows):
    return lax.dynamic_slice_in_dim(block, (lax.axis_index("tm") % 2) * rows, rows, block.ndim - 2)


def after(value, *earlier):
    return lax.optimization_barrier((value, *earlier))[0]


def body(video, conv_taps, modulation, w_qkv, w_out, w_up, w_down):
    frames_in = video[0]
    tap_set = conv_taps[0]
    mod_table = modulation[0]
    frames, tokens = frames_in.shape[:2]
    n_space = lax.axis_size("space")
    qkv_own = w_qkv[0].transpose(1, 2, 0)
    out_own = w_out[0]
    up_own = w_up[0].T
    down_own = w_down[0]

    half = qkv_own.shape[1] // 2
    place, members = lax.axis_index("tm"), lax.axis_size("tm")
    share = up_own.shape[0] // members

    earlier = shifted(frames_in, "tm", 1)
    core = place % 2
    out_share = out_own.shape[0] // (members - 2)
    mine = lax.dynamic_slice_in_dim(
        out_own, jnp.minimum(place, members - 3) * out_share, out_share, 0
    )
    out_rows = lax.all_to_all(
        jnp.broadcast_to(mine[None], (n_space, out_share, D)), "space", 0, 0, tiled=True
    )
    out_rows = out_rows.reshape(n_space * out_share, D)
    out_turned = [out_rows]
    for k in range(1, members // 2):
        out_turned.append(turn_z(out_rows, k))
    near = core_half(qkv_own, half)
    near = flip(near, "space")
    near_more = flip(near, "tm")
    halves = [jnp.where(core == 0, near, near_more), jnp.where(core == 0, near_more, near)]
    near = jnp.concatenate(halves, axis=1)
    far = jnp.concatenate(
        [lax.dynamic_slice_in_dim(w, place * share, share, 0) for w in (up_own, down_own)], axis=0
    )
    far = rotate(far, "space", n_space // 2)

    extended = jnp.concatenate([earlier, frames_in], axis=0).astype(F32)
    mixed_rows = (
        extended[2:]
        + tap_set[0] * extended[2:]
        + tap_set[1] * extended[1:-1]
        + tap_set[2] * extended[:-2]
    ).astype(BF16)
    mixed_f32 = mixed_rows.astype(F32)

    attn_in = modulated(mixed_f32, mod_table[0], mod_table[1])
    outgoing = jnp.broadcast_to(attn_in[None], (n_space // frames, frames, tokens, D))
    rows = lax.all_to_all(outgoing.reshape(n_space, tokens, D), "space", 0, 0, tiled=True)
    rows = rows.reshape(n_space * tokens, D)
    own_heads, near_heads = attend(rows, qkv_own.reshape(-1, D), near.reshape(-1, D))
    odd = lax.axis_index("space") % 2 == 1
    pair = [jnp.where(odd, near_heads, own_heads), jnp.where(odd, own_heads, near_heads)]
    pair = jnp.concatenate(pair, axis=1).reshape(n_space, tokens, -1)
    parts = lax.all_to_all(pair, "space", 0, 0, tiled=True)

    out_turned = lax.optimization_barrier((*out_turned, own_heads))[:-1]
    out_mine = jnp.zeros((members // 2, n_space * out_share, D), BF16)
    for k, rows_k in enumerate(out_turned):
        out_mine = lax.dynamic_update_slice_in_dim(
            out_mine, rows_k[None], (place // 2 - k) % (members // 2), 0
        )
    out_other = flip(out_mine, "tm")
    far = after(far, own_heads)
    turned = [far]
    for k in range(1, members // 2):
        turned.append(turn_z(far, k))
    far = jnp.stack(turned)
    by_core = [jnp.where(core == 0, out_mine, out_other), jnp.where(core == 0, out_other, out_mine)]
    out_all = jnp.stack([w[: members // 2 - 1].reshape(-1, n_space, out_share, D) for w in by_core])
    out_all = out_all.transpose(2, 1, 0, 3, 4).reshape(n_space // frames, -1, D)
    parts = parts.reshape(n_space // frames, frames, tokens, -1)
    attn_sum = jnp.einsum("jftc,jcd->ftd", parts, out_all, preferred_element_type=F32)
    hidden_state = mixed_f32 + mod_table[2] * attn_sum
    mlp_in = modulated(hidden_state, mod_table[3], mod_table[4])
    far_more = flip(far, "tm")
    up_all = jnp.concatenate([up_own] + [w[:, :share].reshape(-1, D) for w in (far, far_more)])
    down_all = jnp.concatenate([down_own] + [w[:, share:].reshape(-1, D) for w in (far, far_more)])

    moves = (2, 1, -1)
    visits = [mlp_in]
    for move in moves:
        visits.append(mirrored(mlp_in, move))
    part = feed_forward(jnp.stack(visits).reshape(-1, D), up_all, down_all)
    part = part.astype(BF16).reshape(-1, frames, tokens, D)
    mlp_sum = part[0].astype(F32)
    for k, move in enumerate(moves):
        mlp_sum = mlp_sum + mirrored(part[k + 1], -move).astype(F32)
    layer_out = (hidden_state + mod_table[5] * mlp_sum).astype(BF16)

    sections = lax.axis_size("section")
    place_x = lax.axis_index("section") % 4
    along_x = [(s, s // 4 * 4 + (s + 1) % 4) for s in range(sections)]

    def crossing(block, x):
        return lax.ppermute(block, "section", [(s, (s + 4) % sections) for s in range(x, sections, 4)])

    second = lax.ppermute(layer_out[1], "section", along_x)
    crossed = crossing(layer_out[0], 3)
    first = lax.ppermute(layer_out[0], "section", [(s, d) for s, d in along_x if d == s + 1])
    crossed_second = crossing(second, 0)
    first_end = lax.ppermute(crossed, "section", [(s, d) for s, d in along_x if d != s + 1])
    arrived = [jnp.where(place_x == 0, first_end, first), jnp.where(place_x == 0, crossed_second, second)]
    return jnp.stack(arrived)[None]


def solution(mesh):
    placed = (
        P("section", "tm", "space", None),
        P("section", None, None),
        P("section", None, None),
        P("section", None, None, "space"),
        P("section", "space", None),
        P("section", None, "space"),
        P("section", "space", None),
    )

    return jax.shard_map(
        body,
        mesh=mesh,
        in_specs=placed,
        out_specs=P("section", "tm", "space", None),
        check_vma=False,
    )
```

```python
import math

import jax
import jax.numpy as jnp
from jax import lax
from jax.experimental import pallas as pl
from jax.experimental.pallas import tpu as pltpu
from jax.sharding import PartitionSpec as P

D = 1152
HEADS = 16
HEAD = D // HEADS
BF16 = jnp.bfloat16
F32 = jnp.float32


def shifted(value, axis, steps):
    count = lax.axis_size(axis)
    initial, last = (max(0, -steps), min(count, count - steps))
    return lax.ppermute(value, axis, [(source, source + steps) for source in range(initial, last)])


def rotate(block, axis, steps):
    count = lax.axis_size(axis)
    return lax.ppermute(block, axis, [(i, (i + steps) % count) for i in range(count)])


def flip(block, axis):
    return lax.ppermute(block, axis, [(i, i ^ 1) for i in range(lax.axis_size(axis))])


def mirrored(block, steps):
    members, count = lax.axis_size("tm"), lax.axis_size("space")
    route = [
        (t * count + y, t * count + (y + (steps if t % 2 == 0 else -steps)) % count)
        for t in range(members)
        for y in range(count)
    ]
    return lax.ppermute(block, ("tm", "space"), route)


def turn_z(block, steps):
    count = lax.axis_size("tm")
    return lax.ppermute(block, "tm", [(i, (i + 2 * steps) % count) for i in range(count)])


def normalize(values_in):
    centre = jnp.mean(values_in, axis=-1, keepdims=True)
    variance = jnp.mean(jnp.square(values_in - centre), axis=-1, keepdims=True)
    return (values_in - centre) * lax.rsqrt(variance + 1e-06)


def modulated(values_in, shift_row, scale_row):
    return (normalize(values_in) * (1.0 + scale_row) + shift_row).astype(BF16)


def mixing_kernel(earlier_ref, frames_ref, taps_ref, mod_ref, mixed_ref, outgoing_ref):
    frames = [earlier_ref[0], earlier_ref[1], frames_ref[0], frames_ref[1]]
    frames = [frame.astype(F32) for frame in frames]
    for f in range(2):
        current, previous, second = frames[f + 2], frames[f + 1], frames[f]
        mixed = (
            current + taps_ref[0:1] * current + taps_ref[1:2] * previous + taps_ref[2:3] * second
        ).astype(BF16)
        mixed_ref[f] = mixed
        attn_in = modulated(mixed.astype(F32), mod_ref[0:1], mod_ref[1:2])
        for k in range(outgoing_ref.shape[0]):
            outgoing_ref[k, f] = attn_in


def attention_kernel(rows_ref, own_ref, own_out_ref, near_ref, part_ref, heads_ref):
    rows = rows_ref[...]
    columns = own_out_ref.shape[0]
    total = None
    for side in range(2):
        qkv_w = own_ref[...] if side == 0 else near_ref[: 3 * columns]
        out_w = own_out_ref[...] if side == 0 else near_ref[3 * columns :]
        projected = lax.dot_general(
            qkv_w, rows, (((1,), (1,)), ((), ())), preferred_element_type=F32
        )
        for head in range(columns // HEAD):
            q, k, v = (
                projected[c * columns + head * HEAD : c * columns + (head + 1) * HEAD].astype(BF16)
                for c in range(3)
            )
            scores = lax.dot_general(k, q, (((0,), (0,)), ((), ())), preferred_element_type=F32)
            top = jnp.max(scores, axis=0, keepdims=True)
            weight = jnp.exp((scores - top) * (1.0 / math.sqrt(HEAD)))
            mass = jnp.sum(weight, axis=0, keepdims=True)
            mixed = jnp.dot(v, weight.astype(BF16), preferred_element_type=F32)
            heads_ref[head * HEAD : (head + 1) * HEAD] = mixed / mass
        part = lax.dot_general(
            heads_ref[...].astype(BF16), out_w, (((0,), (0,)), ((), ())), preferred_element_type=F32
        )
        total = part if total is None else total + part
    part_ref[...] = total.astype(BF16)


def attend(rows, qkv_own, out_own, near):
    tokens, columns = rows.shape[0], out_own.shape[0]
    return pl.pallas_call(
        attention_kernel,
        out_shape=jax.ShapeDtypeStruct((tokens, D), BF16),
        scratch_shapes=[pltpu.VMEM((columns, tokens), F32)],
        name="frame_attention",
    )(rows, qkv_own, out_own, near)


def feed_forward(rows, up_w, down_w):
    activated = jax.nn.gelu(
        jnp.einsum("te,ne->tn", rows, up_w, preferred_element_type=F32), approximate=True
    ).astype(BF16)
    return jnp.dot(activated, down_w, preferred_element_type=F32)


def core_half(block, rows):
    return lax.dynamic_slice_in_dim(block, (lax.axis_index("tm") % 2) * rows, rows, block.ndim - 2)


def after(value, *earlier):
    return lax.optimization_barrier((value, *earlier))[0]


def body(video, conv_taps, modulation, w_qkv, w_out, w_up, w_down):
    frames_in = video[0]
    tap_set = conv_taps[0]
    mod_table = modulation[0]
    frames, tokens = frames_in.shape[:2]
    n_space = lax.axis_size("space")
    qkv_own = w_qkv[0].transpose(1, 2, 0)
    out_own = w_out[0]
    up_own = w_up[0].T
    down_own = w_down[0]

    half = qkv_own.shape[1] // 2
    place, members = lax.axis_index("tm"), lax.axis_size("tm")
    share = up_own.shape[0] // members

    earlier = shifted(frames_in, "tm", 1)
    near = jnp.concatenate([core_half(qkv_own, half), core_half(out_own, half)[None]], axis=0)
    near = flip(near, "space")
    near_more = flip(near, "tm")
    near = jnp.concatenate([near, near_more], axis=1)
    far = jnp.concatenate(
        [lax.dynamic_slice_in_dim(w, place * share, share, 0) for w in (up_own, down_own)], axis=0
    )
    far = rotate(far, "space", n_space // 2)

    mixed_rows, outgoing = pl.pallas_call(
        mixing_kernel,
        out_shape=[
            jax.ShapeDtypeStruct(frames_in.shape, BF16),
            jax.ShapeDtypeStruct((n_space // frames, frames, tokens, D), BF16),
        ],
        name="mix_and_norm",
    )(earlier, frames_in, tap_set, mod_table)
    mixed_f32 = mixed_rows.astype(F32)
    rows = lax.all_to_all(outgoing.reshape(n_space, tokens, D), "space", 0, 0, tiled=True)
    rows = rows.reshape(n_space * tokens, D)
    attn_part = attend(rows, qkv_own.reshape(-1, D), out_own, near.reshape(-1, D))
    attn_part = attn_part.reshape(n_space, tokens, D)
    far = after(far, attn_part)
    turned = [far]
    for k in range(1, members // 2):
        turned.append(turn_z(far, k))
    far = jnp.stack(turned)
    parts = lax.all_to_all(attn_part, "space", 0, 0, tiled=True)
    attn_sum = jnp.sum(parts.reshape(n_space // frames, frames, tokens, D).astype(F32), axis=0)
    hidden_state = mixed_f32 + mod_table[2] * attn_sum
    mlp_in = modulated(hidden_state, mod_table[3], mod_table[4])
    far_more = flip(far, "tm")
    up_all = jnp.concatenate([up_own] + [w[:, :share].reshape(-1, D) for w in (far, far_more)])
    down_all = jnp.concatenate([down_own] + [w[:, share:].reshape(-1, D) for w in (far, far_more)])

    moves = (2, 1, -1)
    visits = [mlp_in]
    for move in moves:
        visits.append(mirrored(mlp_in, move))
    part = feed_forward(jnp.stack(visits).reshape(-1, D), up_all, down_all)
    part = part.astype(BF16).reshape(-1, frames, tokens, D)
    mlp_sum = part[0].astype(F32)
    for k, move in enumerate(moves):
        mlp_sum = mlp_sum + mirrored(part[k + 1], -move).astype(F32)
    layer_out = (hidden_state + mod_table[5] * mlp_sum).astype(BF16)

    sections = lax.axis_size("section")
    place_x = lax.axis_index("section") % 4
    along_x = [(s, s // 4 * 4 + (s + 1) % 4) for s in range(sections)]
    layer_out = layer_out.reshape(-1, D)
    cut = layer_out.shape[0] // 2

    def crossing(block, x):
        return lax.ppermute(block, "section", [(s, (s + 4) % sections) for s in range(x, sections, 4)])

    second = lax.ppermute(layer_out[cut:], "section", along_x)
    crossed = crossing(layer_out[:cut], 3)
    first = lax.ppermute(layer_out[:cut], "section", [(s, d) for s, d in along_x if d == s + 1])
    crossed_second = crossing(second, 0)
    first_end = lax.ppermute(crossed, "section", [(s, d) for s, d in along_x if d != s + 1])
    first = jnp.where(place_x == 0, first_end, first)
    second = jnp.where(place_x == 0, crossed_second, second)
    return jnp.concatenate([first, second]).reshape(video.shape)


def solution(mesh):
    placed = (
        P("section", "tm", "space", None),
        P("section", None, None),
        P("section", None, None),
        P("section", None, None, "space"),
        P("section", "space", None),
        P("section", None, "space"),
        P("section", "space", None),
    )

    return jax.shard_map(
        body,
        mesh=mesh,
        in_specs=placed,
        out_specs=P("section", "tm", "space", None),
        check_vma=False,
    )
```
